32 devices in a mesh: runs: 2 (over y), ctx: 4 (over z), head: 4 (over x, core).
Axes of the slice: x: 2, y: 2, z: 4, core: 2. Of those that a mesh axis runs over, the one named last changes fastest.
Arguments:
- tokens: bfloat16 [4096, 2048], P(('runs', 'ctx', 'head')), parts along dimension 0, may hold values from -400 to 400
- in_gain: float32 [2048], replicated, may hold values from 0.1 to 1.9
- projections: bfloat16 [3, 2048, 2048], P(None, 'ctx', 'head'), may hold values from -0.125 to 0.125
- prior_state: float32 [32, 128, 128], P(('runs', 'head')), parts along dimension 0, may hold values from -256 to 256
- out_gain: float32 [2048], P('head'), may hold values from 0.1 to 1.9
Outputs:
- attended: bfloat16 [4096, 2048], P(('runs', 'ctx', 'head')), parts along dimension 0
The draws below stay inside these ranges and needn't reach their ends.
There are 2 independent parts, one for each index of `runs`. The reference program is written for one: setup_inputs(seed, part) draws one part's arguments, and reference() takes and returns one part's arrays. A program takes and returns all parts, laid end to end along the dimension named above; an argument that names none is the same for every part. Nothing has to cross between parts.
All inputs are finite; a program needn't handle non-finite values.
Results may differ from the reference program's by a relative error of at most 0.0071.
Values may be sent and summed in bfloat16 or wider, within the bound.
A program may use at most 64 MiB of HBM per device.

```python
import math
import jax
import jax.numpy as jnp
from jax import lax

D = 2048
HEADS = 16
HEAD_DIM = 128
BLOCK = 512
SEQ = 2048


def draw_tokens(key, part):
    first, second, third = jax.random.split(key, 3)
    row_scale = jnp.exp(jax.random.uniform(first, (SEQ, 1), jnp.float32, 0.0, math.log(10.0)))
    col_scale = jnp.exp(jax.random.uniform(second, (1, D), jnp.float32, 0.0, math.log(10.0)))
    base = jnp.clip(jax.random.normal(third, (SEQ, D), jnp.float32), -4.0, 4.0)
    return (base * row_scale * col_scale).astype(jnp.bfloat16)


def steps_of(key, extent, pieces, least, top_value):
    level = 1.0
    for dim, blocks in pieces:
        heights = jax.random.uniform(jax.random.fold_in(jax.random.fold_in(key, 6), dim), (blocks,), jnp.float32, least / len(pieces), top_value / len(pieces))
        level = level * jnp.repeat(jnp.exp(heights), extent[dim] // blocks).reshape((-1,) + (1,) * (len(extent) - 1 - dim))
    return level


def gaussian(key, extent, scale, reach, cuts=(), kind=jnp.bfloat16):
    values = jax.random.normal(key, extent, jnp.float32) * scale
    if len(cuts) > 0:
        values = steps_of(key, extent, cuts, -0.22, 0.18) * values
    return jnp.clip(values, min=-reach, max=reach).astype(kind)


def setup_inputs(seed: int = 0, part: int = 0) -> dict:
    key_of = jax.random.split(jax.random.key(seed), 6)
    part_splits = jax.random.split(jax.random.fold_in(key_of[5], part), 6)
    return {
        "tokens": draw_tokens(jax.random.fold_in(jax.random.fold_in(key_of[5], part), 71), part),
        "in_gain": jnp.clip(1.0 + 0.18 * jax.random.normal(key_of[1], (D,), jnp.float32), 0.1, 1.9),
        "projections": gaussian(key_of[2], (3, D, D), D ** -0.5, 0.125, ((1, 4), (2, 4))),
        "prior_state": gaussian(part_splits[3], (HEADS, HEAD_DIM, HEAD_DIM), (SEQ ** 0.5), 256.0, ((0, 4),), jnp.float32),
        "out_gain": jnp.clip(1.0 + 0.18 * jax.random.normal(key_of[4], (D,), jnp.float32), 0.1, 1.9),
    }


def rms_tokens(values_in, gain):
    wide = values_in.astype(jnp.float32)
    scale = lax.rsqrt(lax.optimization_barrier(jnp.mean(wide * wide, axis=-1, keepdims=True)) + 1e-06)
    return (wide * scale * gain).astype(jnp.bfloat16)

def reference(tokens, in_gain, projections, prior_state, out_gain):
    normed = rms_tokens(tokens, in_gain)
    queries = jnp.dot(normed, projections[0], preferred_element_type=jnp.float32).astype(jnp.bfloat16)
    keys_all = jnp.dot(normed, projections[1], preferred_element_type=jnp.float32).astype(jnp.bfloat16)
    values_all = jnp.dot(normed, projections[2], preferred_element_type=jnp.float32).astype(jnp.bfloat16)
    count = SEQ // BLOCK
    queries = queries.reshape(count, BLOCK, HEADS, HEAD_DIM)
    keys_all = keys_all.reshape(count, BLOCK, HEADS, HEAD_DIM)
    values_all = values_all.reshape(count, BLOCK, HEADS, HEAD_DIM)
    position = jnp.arange(BLOCK, dtype=jnp.int32)
    causal = position[:, None] >= position[None, :]
    gains = out_gain.reshape(HEADS, HEAD_DIM)

    def advance(state, block_in):
        query_blk, key_blk, value_blk = block_in
        query_f = query_blk.astype(jnp.float32)
        key_f = key_blk.astype(jnp.float32)
        value_f = value_blk.astype(jnp.float32)
        scores = jnp.einsum('qhd,khd->hqk', query_f, key_f)
        scores = jnp.where(causal[None], scores, 0.0)
        rounded = lax.optimization_barrier(scores.astype(jnp.bfloat16)).astype(jnp.float32)
        intra = jnp.einsum('hqk,khd->qhd', rounded, value_f)
        state_low = lax.optimization_barrier(state.astype(jnp.bfloat16)).astype(jnp.float32)
        inter = jnp.einsum('qhd,hde->qhe', query_f, state_low)
        mixed = intra + inter
        scale = lax.rsqrt(lax.optimization_barrier(jnp.mean(mixed * mixed, axis=-1, keepdims=True)) + 1e-06)
        result = (mixed * scale * gains).astype(jnp.bfloat16).reshape(BLOCK, HEADS * HEAD_DIM)
        state = state + jnp.einsum('khd,khe->hde', key_f, value_f)
        return (state, result)
    _, outputs = lax.scan(advance, prior_state.astype(jnp.float32), (queries, keys_all, values_all))
    return outputs.reshape(SEQ, HEADS * HEAD_DIM)
```

```python
import functools

import jax
import jax.numpy as jnp
from jax import lax
from jax.experimental import pallas as pl
from jax.experimental.pallas import tpu as pltpu
from jax.sharding import PartitionSpec as P

BLOCK = 512
CORES = 2
MESH = pl.DeviceIdType.MESH
QUERY, KEY, VALUE = 0, 1, 2
TILE = 256
CUTS = 1
TOKEN_CUTS = 4
WIDE_TILE = 512
PRM = dict(
    l_at_heavy=9, l_at_light=3, full=3, token_gap=3, h_token_gap=1,
)
TIMES = {
    "H": {
        "A": (5.2, 6.6, 8.0, 19.3, 20.7, 22.1, 26.4, 29.2, 32.9,),
        "B": (2.9, 4.3, 5.7, 7.1, 8.5, 9.9, 11.3, 13.8, 16.6,),
        "C": (24.0, 25.4, 26.8, 28.2, 29.6, 31.8, 33.0, 34.6, 38.8,),
        "KV": (30.3, 33.1, 37.3,),
        "O1": (36.3, 39.5, 42.3,),
        "Q": (31.9, 34.7, 41.3,),
        "TF": (15.1, 18.1, 21.9, 28.9,),
        "TP": (3.8, 10.9, 17.9, 25.0,),
        "TX": (4.0, 6.8, 9.5, 12.3,),
    },
    "L": {
        "KV": (27.1,),
        "LH": (21.8, 23.6, 25.0,),
        "LL": (15.1, 17.9, 22.1,),
        "LP": (14.7, 17.6, 20.4,),
        "O1": (37.3,),
        "Q": (28.6,),
        "TF": (15.2, 18.0, 20.8, 23.7,),
        "TP": (3.8, 6.6, 9.5, 12.3,),
        "TX": (4.0, 6.8, 9.6, 12.4,),
    },
}


def dot(a, b, contract=((1,), (0,))):
    return lax.dot_general(a, b, (contract, ((), ())), preferred_element_type=jnp.float32)


def kernel(
    n_ctx, n_head,
    tok_hbm, gain_hbm, w_ref, prior_hbm, og_hbm,
    out_ref,
    tok_ref, gain_ref, prior_ref, og_ref, in_sems,
    x_buf, kv_w, q_w, kv_buf, q_buf, att, sums, totals, others, starts,
    own_sem, tz_send, tz_recv, tx_send, tx_recv, tc_send, tc_recv,
    wz_send, wz_recv, wr_send, wy_send, wy_recv, st_send, st_recv, o_send, o_recv, o_own,
):
    run = lax.axis_index("runs")
    z = lax.axis_index("ctx")
    h = lax.axis_index("head")
    n_x = n_head // CORES
    x, core = h // CORES, h % CORES
    half = z % 2
    pair = z // 2
    n_pairs = n_ctx // 2
    partner = z + 1 - 2 * half
    other_run = {"runs": 1 - run}
    rows_here = tok_ref.shape[0]
    rows = w_ref.shape[1]
    rows_half = rows // 2
    cuts = CUTS
    rows_cut = rows_half // cuts
    heads_here, dim, _ = prior_ref.shape
    n_heavy = kv_w.shape[0]
    n_light = heads_here - n_heavy
    n_tok = x_buf.shape[0]
    span = n_tok // 2
    per_span = span // BLOCK
    tok_cut = rows_here // TOKEN_CUTS

    is_light = half == pair % 2

    def light_of(q):
        return 2 * q + q % 2

    def heavy_of(q):
        return 2 * q + 1 - q % 2

    def later_pair(k):
        return (pair + k) % n_pairs

    L_HEADS = list(range(n_light))
    H_HEADS = list(range(n_light, heads_here))
    L_STAGES = [(g, j, c) for g in L_HEADS for j in (KEY, VALUE, QUERY) for c in range(cuts)]
    H_STAGES = [(g, j, c) for g in H_HEADS for j in (KEY, VALUE, QUERY) for c in range(cuts)]

    def unit(g):
        return g if g < n_light else g - n_light

    def index(stage):
        g, j, c = stage
        return (g * 3 + j) * cuts + c

    def in_full(stage):
        return n_heavy > 1 and H_STAGES.index(stage) >= (n_heavy * 3 - PRM["full"]) * cuts

    def slot(side, head):
        return pl.ds(pl.multiple_of((side * n_head + head) * rows_here, rows_here), rows_here)

    def token_piece(side, head, i):
        start = (side * n_head + head) * rows_here + i * tok_cut
        return x_buf.at[pl.ds(pl.multiple_of(start, tok_cut), tok_cut), :]

    def source(stage, part):
        g, j, c = stage
        start = pl.multiple_of(part * rows_half + c * rows_cut, rows_cut)
        return w_ref.at[j, pl.ds(start, rows_cut), pl.ds(g * dim, dim)]

    def place(g, j, at):
        u = unit(g)
        if j == QUERY:
            return q_w.at[u, at, :]
        return kv_w.at[u, at, pl.ds((j - KEY) * dim, dim)]

    def piece(stage, src, part):
        g, j, c = stage
        start = pl.multiple_of(src * rows + part * rows_half + c * rows_cut, rows_cut)
        return place(g, j, pl.ds(start, rows_cut))

    loads = [
        pltpu.make_async_copy(src, dst, in_sems.at[n])
        for n, (src, dst) in enumerate((
            (tok_hbm, tok_ref), (gain_hbm, gain_ref), (prior_hbm, prior_ref), (og_hbm, og_ref),
        ))
    ]
    for load in loads:
        load.start()

    barrier = pltpu.get_barrier_semaphore()
    greeted = [other_run]
    greeted += [{"ctx": (z + k) % n_ctx} for k in range(1, n_ctx)]
    greeted += [{"head": (h + k) % n_head} for k in range(1, n_head)]
    greeted += [{"ctx": partner, "head": (h + k) % n_head} for k in range(1, n_head)]
    for device in greeted:
        pl.semaphore_signal(barrier, inc=1, device_id=device, device_id_type=MESH)

    loads[0].wait()
    loads[1].wait()
    wide = tok_ref[...].astype(jnp.float32)
    scale = lax.rsqrt(jnp.mean(wide * wide, axis=-1, keepdims=True) + 1e-06)
    x_buf[slot(half, h), :] = (wide * scale * gain_ref[...]).astype(jnp.bfloat16)
    pl.semaphore_wait(barrier, len(greeted))

    def remote(src, dst, send_sem, recv_sem, device):
        return pltpu.make_async_remote_copy(
            src_ref=src, dst_ref=dst, send_sem=send_sem, recv_sem=recv_sem,
            device_id=device, device_id_type=MESH,
        )

    def arrived(dst, recv_sem):
        remote(dst, dst, own_sem, recv_sem, other_run).wait_recv()

    def whole_program(light):
        my_heads = L_HEADS if light else H_HEADS
        my_stages = L_STAGES if light else H_STAGES
        sent = []
        steps = []

        def send(*what):
            copy = remote(*what)
            copy.start()
            sent.append(copy)

        own_w = [
            pltpu.make_async_copy(
                w_ref.at[j, :, pl.ds(g * dim, dim)],
                place(g, j, pl.ds(pl.multiple_of(z * rows, rows), rows)),
                in_sems.at[4 + unit(g) * 3 + j],
            )
            for g in my_heads for j in (KEY, VALUE, QUERY)
        ]

        def spread(side, b, i):
            block = token_piece(side, h, i)
            for d in range(1, n_x):
                send(block, block, tx_send.at[d, b, i], tx_recv.at[d, b, i],
                     {"head": ((x + d) % n_x) * CORES + core})
            send(block, block, tc_send.at[0, b, i], tc_recv.at[0, b, i],
                 {"head": x * CORES + 1 - core})

        def token_to_partner(i):
            block = token_piece(half, h, i)
            send(block, block, tz_send.at[i], tz_recv.at[i], {"ctx": partner})

        def partner_tokens(i):
            arrived(token_piece(1 - half, h, i), tz_recv.at[i])
            spread(1 - half, 1, i)

        def pass_on(side, b, i):
            for d in range(1, n_x):
                block = token_piece(side, ((x + n_x - d) % n_x) * CORES + core, i)
                arrived(block, tx_recv.at[d, b, i])
                send(block, block, tc_send.at[d, b, i], tc_recv.at[d, b, i],
                     {"head": x * CORES + 1 - core})

        def wait_tokens():
            for b, side in ((0, half), (1, 1 - half)):
                for d in range(n_x):
                    head = ((x + n_x - d) % n_x) * CORES + 1 - core
                    for i in range(TOKEN_CUTS):
                        arrived(token_piece(side, head, i), tc_recv.at[d, b, i])

        def send_stage(stage):
            s = index(stage)
            src = source(stage, run)
            dst = piece(stage, z, run)
            to_light = stage[0] < n_light
            if to_light and not light:
                send(src, dst, wz_send.at[s, 0], wz_recv.at[s, z], {"ctx": partner})
            if not to_light and light:
                send(src, dst, wz_send.at[s, 0], wz_recv.at[s, z], {"ctx": partner})
                if in_full(stage):
                    send(source(stage, 1 - run), piece(stage, z, 1 - run),
                         wy_send.at[s, z], wy_recv.at[s, z], {"ctx": partner})
                return
            for k in range(1, n_pairs):
                to = light_of(later_pair(k)) if to_light else heavy_of(later_pair(k))
                send(src, dst, wz_send.at[s, k], wz_recv.at[s, z], {"ctx": to})

        def take(stage, src, relay=False, swap=True):
            s = index(stage)
            block = piece(stage, src, run)
            arrived(block, wz_recv.at[s, src])
            if relay:
                for k in range(1, n_pairs):
                    send(block, block, wr_send.at[s, k], wz_recv.at[s, src],
                         {"ctx": heavy_of(later_pair(k))})
            if swap:
                send(block, block, wy_send.at[s, src], wy_recv.at[s, src], other_run)

        def wait_weights(g, j):
            for c in range(cuts):
                s = index((g, j, c))
                for k in range(1, n_ctx):
                    src = (z + k) % n_ctx
                    arrived(piece((g, j, c), src, 1 - run), wy_recv.at[s, src])

        def project(a_ref, b_ref, to_ref):
            def tile(step, carry):
                at = pl.ds(pl.multiple_of(step * WIDE_TILE, WIDE_TILE), WIDE_TILE)
                to_ref[at, :] = dot(a_ref[at, :], b_ref[...]).astype(jnp.bfloat16)
                return carry

            lax.fori_loop(0, n_tok // WIDE_TILE, tile, 0)

        def keys_values(g):
            u = unit(g)
            wait_weights(g, KEY)
            wait_weights(g, VALUE)
            own_w[u * 3].wait()
            own_w[u * 3 + 1].wait()
            project(x_buf, kv_w.at[u], kv_buf.at[u])
            total = None
            for b in range(n_tok // BLOCK):
                here = pl.ds(b * BLOCK, BLOCK)
                one = dot(kv_buf[u, here, :dim], kv_buf[u, here, dim:], ((0,), (0,)))
                sums[u, b] = one
                total = one if total is None else total + one
            totals[u] = total
            for k in range(1, n_pairs):
                @pl.when(pair + k < n_pairs)
                def _():
                    to = light_of(pair + k) if light else heavy_of(pair + k)
                    remote(totals.at[u], others.at[k, u], st_send.at[k, u], st_recv.at[k, u],
                           {"ctx": to}).start()

        def queries(g):
            u = unit(g)
            wait_weights(g, QUERY)
            own_w[u * 3 + 2].wait()
            project(x_buf, q_w.at[u], q_buf.at[u])

        def states(g):
            u = unit(g)
            for k in range(1, n_pairs):
                @pl.when(pair >= k)
                def _():
                    arrived(others.at[k, u], st_recv.at[k, u])
            state = prior_ref[g]
            for k in range(1, n_pairs):
                state = state + jnp.where(pair >= k, others[k, u], 0.0)
            for b in range(n_tok // BLOCK):
                starts[u, b] = state.astype(jnp.bfloat16)
                state = state + sums[u, b]

        def attend(g, side, bb, r):
            u = unit(g)
            b = side * per_span + bb
            base = pl.multiple_of(b * BLOCK, BLOCK)
            seen = r + TILE
            here = pl.ds(pl.multiple_of(base + r, TILE), TILE)
            before = pl.ds(base, seen)
            row = lax.broadcasted_iota(jnp.int32, (TILE, seen), 0) + r
            col = lax.broadcasted_iota(jnp.int32, (TILE, seen), 1)
            query = q_buf[u, here, :]
            scores = dot(query, kv_buf[u, before, :dim], ((1,), (1,)))
            scores = jnp.where(row >= col, scores, 0.0).astype(jnp.bfloat16)
            mixed = dot(scores, kv_buf[u, before, dim:]) + dot(query, starts[u, b])
            level = lax.rsqrt(jnp.mean(mixed * mixed, axis=-1, keepdims=True) + 1e-06)
            att[u, here, :] = (mixed * level * og_ref[g]).astype(jnp.bfloat16)

        def columns(head, g):
            return out_ref.at[:, pl.ds(pl.multiple_of((head * heads_here + g) * dim, dim), dim)]

        def outputs(g):
            u = unit(g)
            for bb in range(per_span):
                for r in range(0, BLOCK, TILE):
                    attend(g, 1 - half, bb, r)
                    first = (bb * BLOCK + r) // rows_here
                    for head in range(first, first + TILE // rows_here):
                        send(att.at[u, slot(1 - half, head), :], columns(h, g),
                             o_send.at[u, 1, head], o_recv.at[h, g], {"ctx": partner, "head": head})
            for bb in range(per_span):
                for r in range(0, BLOCK, TILE):
                    attend(g, half, bb, r)
            for dh in range(1, n_head):
                to = (h + dh) % n_head
                send(att.at[u, slot(half, to), :], columns(h, g),
                     o_send.at[u, 0, dh], o_recv.at[h, g], {"head": to})
            pltpu.make_async_copy(att.at[u, slot(half, h), :], columns(h, g), o_own.at[u]).start()

        def step(time, work, *args):
            steps.append((time, len(steps), functools.partial(work, *args)))

        def by_head(g):
            return [s for s in H_STAGES if s[0] == g]

        def order(at):
            at = min(at * cuts, len(H_STAGES))
            return H_STAGES[:at] + L_STAGES + H_STAGES[at:]

        heavy_order, light_order = order(PRM["l_at_heavy"]), order(PRM["l_at_light"])

        def when(name, n, default=0.0):
            times = TIMES["L" if light else "H"].get(name)
            return times[min(n, len(times) - 1)] if times else default

        for n, stage in enumerate(my_stages):
            n = n // cuts
            from_partner = when("LP" if light else "A", n)
            step(from_partner, take, stage, partner, not light,
                 light or not in_full(stage))
            for k in range(1, n_pairs):
                step(when("LH" if light else "B", n), take, stage, heavy_of(later_pair(k)))
                far = when("LL", n) if light else max(when("C", n), from_partner)
                step(far, take, stage, light_of(later_pair(k)))
        last = {}
        for time, _, work in steps:
            key = work.args[0][:2]
            last[key] = max(last.get(key, 0.0), time)
        free = 0.0
        for i in range(TOKEN_CUTS):
            near = when("TP", i)
            far = max(when("TF", i), near)
            step(near, partner_tokens, i)
            step(when("TX", i), pass_on, half, 0, i)
            step(far, pass_on, 1 - half, 1, i)
            free = max(free, far, when("TX", i))
        free = max(free, when("KV", 0))
        step(free, wait_tokens)
        for n, g in enumerate(my_heads):
            free = max(free, when("KV", n), last[g, KEY], last[g, VALUE])
            step(free, keys_values, g)
            free = max(free, when("Q", n), last[g, QUERY])
            step(free, queries, g)
            free = max(free, when("O1", n))
            step(free, states, g)
            step(free, outputs, g)

        for copy in own_w:
            copy.start()
        gap = PRM["token_gap" if light else "h_token_gap"] * cuts
        stages = list(light_order if light else heavy_order)
        for i in range(TOKEN_CUTS):
            token_to_partner(i)
            if i == 0:
                for piece_of in range(TOKEN_CUTS):
                    spread(half, 0, piece_of)
            for _ in range(gap):
                if stages:
                    send_stage(stages.pop(0))
        for stage in stages:
            send_stage(stage)
        loads[2].wait()
        loads[3].wait()
        for _, _, work in sorted(steps, key=lambda s: s[:2]):
            work()

        for dh in range(n_head):
            head = (h + dh) % n_head
            for g in range(heads_here):
                if dh or g not in my_heads:
                    arrived(columns(head, g), o_recv.at[head, g])
        for g in my_heads:
            u = unit(g)
            pltpu.make_async_copy(att.at[u, slot(half, h), :], columns(h, g), o_own.at[u]).wait()
            for k in range(1, n_pairs):
                @pl.when(pair + k < n_pairs)
                def _():
                    remote(totals.at[u], others.at[k, u], st_send.at[k, u], st_recv.at[k, u],
                           other_run).wait_send()
        for copy in sent:
            copy.wait_send()

    @pl.when(is_light)
    def _():
        whole_program(True)

    @pl.when(jnp.logical_not(is_light))
    def _():
        whole_program(False)


def on_device(n_ctx, n_head, tokens, in_gain, projections, prior_state, out_gain):
    rows_here, features = tokens.shape
    heads_here, dim, _ = prior_state.shape
    n_heavy = heads_here - max(1, heads_here // 4)
    n_tok = 2 * n_head * rows_here
    n_blocks = n_tok // BLOCK
    n_x = n_head // CORES
    n_pairs = n_ctx // 2
    n_stages = 3 * heads_here * CUTS
    dma = pltpu.SemaphoreType.DMA
    vmem = pl.BlockSpec(memory_space=pltpu.VMEM)
    bf16, f32 = jnp.bfloat16, jnp.float32
    return pl.pallas_call(
        functools.partial(kernel, n_ctx, n_head),
        out_shape=jax.ShapeDtypeStruct((rows_here, features), bf16),
        in_specs=[pl.BlockSpec(memory_space=pltpu.HBM)] * 5,
        out_specs=vmem,
        scratch_shapes=[
            pltpu.VMEM((rows_here, features), bf16),
            pltpu.VMEM((1, features), f32),
            pltpu.VMEM((heads_here, dim, dim), f32),
            pltpu.VMEM((heads_here, 1, dim), f32),
            dma((4 + 3 * n_heavy,)),
            pltpu.VMEM((n_tok, features), bf16),
            pltpu.VMEM((n_heavy, features, 2 * dim), bf16),
            pltpu.VMEM((n_heavy, features, dim), bf16),
            pltpu.VMEM((n_heavy, n_tok, 2 * dim), bf16),
            pltpu.VMEM((n_heavy, n_tok, dim), bf16),
            pltpu.VMEM((n_heavy, n_tok, dim), bf16),
            pltpu.VMEM((n_heavy, n_blocks, dim, dim), f32),
            pltpu.VMEM((n_heavy, dim, dim), f32),
            pltpu.VMEM((n_pairs, n_heavy, dim, dim), f32),
            pltpu.VMEM((n_heavy, n_blocks, dim, dim), bf16),
            dma,
            dma((TOKEN_CUTS,)), dma((TOKEN_CUTS,)),
            dma((n_x, 2, TOKEN_CUTS)), dma((n_x, 2, TOKEN_CUTS)),
            dma((n_x, 2, TOKEN_CUTS)), dma((n_x, 2, TOKEN_CUTS)),
            dma((n_stages, n_pairs)), dma((n_stages, n_ctx)), dma((n_stages, n_pairs)),
            dma((n_stages, n_ctx)), dma((n_stages, n_ctx)),
            dma((n_pairs, n_heavy)), dma((n_pairs, n_heavy)),
            dma((n_heavy, 2, n_head)), dma((n_head, heads_here)), dma((n_heavy,)),
        ],
        compiler_params=pltpu.CompilerParams(
            collective_id=0, has_side_effects=True, vmem_limit_bytes=60 * 1024 * 1024
        ),
    )(
        tokens,
        in_gain.reshape(1, features),
        projections,
        prior_state,
        out_gain.reshape(heads_here, 1, dim),
    )


def solution(mesh):
    in_specs = (
        P(("runs", "ctx", "head"), None),
        P(),
        P(None, "ctx", "head"),
        P(("runs", "head"), None, None),
        P("head"),
    )
    out_specs = P(("runs", "ctx", "head"), None)
    return jax.shard_map(
        functools.partial(on_device, mesh.shape["ctx"], mesh.shape["head"]),
        mesh=mesh, in_specs=in_specs, out_specs=out_specs, check_vma=False,
    )
```

```python
import functools

import jax
import jax.numpy as jnp
from jax import lax
from jax.experimental import pallas as pl
from jax.experimental.pallas import tpu as pltpu
from jax.sharding import PartitionSpec as P

BLOCK = 512
CORES = 2
MESH = pl.DeviceIdType.MESH
QUERY, KEY, VALUE = 0, 1, 2
TILE = 256
TOKEN_CUTS = 4
WIDE_TILE = 512
STATE = jnp.float32
SENDS = {
    "L": (
        "h0", "N", "T0", "X0", "T1", "X1", "X2", "X3", "h1", "T2", "h2", "T3",
        "h3", "l0", "h4", "h5", "l1", "l2", "h6", "f6", "h7", "f7", "h8", "f8",
    ),
    "H": (
        "h0", "h1", "N", "T0", "X0", "T1", "X1", "T2", "X2", "T3", "X3", "h2",
        "h3", "h4", "h5", "h6", "h7", "h8", "p0", "l0", "p1", "l1", "p2", "l2",
    ),
}
TIMES = {
    "H": {
        "A": (3.6, 10.7, 14.9, 19.1, 21.9, 23.3, 27.6, 31.3, 33.2,),
        "B": (3.7, 5.0, 6.6, 7.8, 9.4, 10.8, 12.1, 13.6, 15.0,),
        "C": (20.9, 23.5, 25.1, 27.9, 31.4, 32.6, 33.3, 37.3, 39.1,),
        "KV": (29.9, 35.9, 41.9,),
        "O1": (34.9, 40.9, 46.9,),
        "Q": (31.5, 37.4, 43.3,),
        "TF": (17.5, 20.3, 23.1, 25.9,),
        "TP": (6.4, 9.2, 13.5, 17.7,),
        "TX": (6.2, 9.0, 11.8, 14.7,),
    },
    "L": {
        "KV": (31.4,),
        "LH": (18.5, 21.3, 23.1,),
        "LL": (24.5, 27.7, 30.5,),
        "LP": (16.0, 18.8, 21.6,),
        "O1": (40.7,),
        "Q": (34.2,),
        "TF": (17.4, 20.2, 23.2, 25.9,),
        "TP": (6.1, 9.0, 11.8, 14.6,),
        "TX": (6.3, 9.1, 11.9, 14.7,),
    },
}


def dot(a, b, contract=((1,), (0,))):
    return lax.dot_general(a, b, (contract, ((), ())), preferred_element_type=jnp.float32)


def kernel(
    n_ctx, n_head,
    tok_hbm, gain_hbm, w_ref, prior_hbm, og_hbm,
    out_ref,
    tok_ref, gain_ref, prior_ref, og_ref, in_sems,
    x_buf, kv_w, q_w, kv_buf, q_buf, att, sums, totals, others, starts,
    own_sem, t_sent, tz_recv, tx_recv, tc_recv,
    w_sent, wz_recv, wy_recv, st_send, st_recv, o_send, o_recv, o_own,
):
    run = lax.axis_index("runs")
    z = lax.axis_index("ctx")
    h = lax.axis_index("head")
    n_x = n_head // CORES
    x, core = h // CORES, h % CORES
    half = z % 2
    pair = z // 2
    n_pairs = n_ctx // 2
    partner = z + 1 - 2 * half
    other_run = {"runs": 1 - run}
    rows_here = tok_ref.shape[0]
    rows = w_ref.shape[1]
    rows_half = rows // 2
    heads_here, dim, _ = prior_ref.shape
    n_heavy = kv_w.shape[0]
    n_light = heads_here - n_heavy
    n_tok = x_buf.shape[0]
    span = n_tok // 2
    per_span = span // BLOCK
    tok_cut = rows_here // TOKEN_CUTS

    is_light = half == pair % 2

    def light_of(q):
        return 2 * q + q % 2

    def heavy_of(q):
        return 2 * q + 1 - q % 2

    def later_pair(k):
        return (pair + k) % n_pairs

    L_HEADS = list(range(n_light))
    H_HEADS = list(range(n_light, heads_here))
    L_STAGES = [(g, j) for g in L_HEADS for j in (KEY, VALUE, QUERY)]
    H_STAGES = [(g, j) for g in H_HEADS for j in (KEY, VALUE, QUERY)]

    def unit(g):
        return g if g < n_light else g - n_light

    def index(stage):
        return stage[0] * 3 + stage[1]

    def group(stage):
        return stage[0] * 2 + (stage[1] == QUERY)

    def in_full(stage):
        return n_heavy > 1 and "f%d" % H_STAGES.index(stage) in SENDS["L"]

    def slot(side, head):
        return pl.ds(pl.multiple_of((side * n_head + head) * rows_here, rows_here), rows_here)

    def token_piece(side, head, i):
        start = (side * n_head + head) * rows_here + i * tok_cut
        return x_buf.at[pl.ds(pl.multiple_of(start, tok_cut), tok_cut), :]

    def source(stage, part):
        g, j = stage
        start = pl.multiple_of(part * rows_half, rows_half)
        return w_ref.at[j, pl.ds(start, rows_half), pl.ds(g * dim, dim)]

    def place(g, j, at):
        u = unit(g)
        if j == QUERY:
            return q_w.at[u, at, :]
        return kv_w.at[u, at, pl.ds((j - KEY) * dim, dim)]

    def piece(stage, src, part):
        start = pl.multiple_of(src * rows + part * rows_half, rows_half)
        return place(*stage, pl.ds(start, rows_half))

    loads = [
        pltpu.make_async_copy(src, dst, in_sems.at[n])
        for n, (src, dst) in enumerate((
            (tok_hbm, tok_ref), (gain_hbm, gain_ref), (prior_hbm, prior_ref), (og_hbm, og_ref),
        ))
    ]
    for load in loads:
        load.start()

    barrier = pltpu.get_barrier_semaphore()
    greeted = [other_run]
    greeted += [{"ctx": (z + k) % n_ctx} for k in range(1, n_ctx)]
    greeted += [{"head": (h + k) % n_head} for k in range(1, n_head)]
    greeted += [{"ctx": partner, "head": (h + k) % n_head} for k in range(1, n_head)]
    for device in greeted:
        pl.semaphore_signal(barrier, inc=1, device_id=device, device_id_type=MESH)

    pl.semaphore_wait(barrier, len(greeted))

    def normalize():
        loads[0].wait()
        loads[1].wait()
        wide = tok_ref[...].astype(jnp.float32)
        scale = lax.rsqrt(jnp.mean(wide * wide, axis=-1, keepdims=True) + 1e-06)
        x_buf[slot(half, h), :] = (wide * scale * gain_ref[...]).astype(jnp.bfloat16)

    def remote(src, dst, send_sem, recv_sem, device):
        return pltpu.make_async_remote_copy(
            src_ref=src, dst_ref=dst, send_sem=send_sem, recv_sem=recv_sem,
            device_id=device, device_id_type=MESH,
        )

    def arrived(dst, recv_sem):
        remote(dst, dst, own_sem, recv_sem, other_run).wait_recv()

    sent_sems = {"tokens": t_sent, "weights": w_sent}

    def whole_program(light):
        my_heads = L_HEADS if light else H_HEADS
        my_stages = L_STAGES if light else H_STAGES
        steps = []
        n_sent = {"tokens": 0, "weights": 0}

        def send(src, dst, kind, recv_sem, device):
            remote(src, dst, sent_sems[kind], recv_sem, device).start()
            n_sent[kind] += 1

        def wait_sent(kind, ref):
            copies = n_sent[kind] * (ref.shape[0] * ref.shape[1])
            whole = copies // x_buf.shape[1]
            if whole <= n_tok and whole % 16 == 0 and whole * x_buf.shape[1] == copies:
                ref, times = x_buf.at[pl.ds(0, whole), :], 1
            else:
                times = n_sent[kind]
            for _ in range(times):
                remote(ref, ref, sent_sems[kind], own_sem, other_run).wait_send()

        own_w = [
            pltpu.make_async_copy(
                w_ref.at[j, :, pl.ds(g * dim, dim)],
                place(g, j, pl.ds(pl.multiple_of(z * rows, rows), rows)),
                in_sems.at[4 + unit(g) * 3 + j],
            )
            for g in my_heads for j in (KEY, VALUE, QUERY)
        ]

        def spread(side, b, i):
            block = token_piece(side, h, i)
            for d in range(1, n_x):
                send(block, block, "tokens", tx_recv.at[d, b, i],
                     {"head": ((x + d) % n_x) * CORES + core})
            send(block, block, "tokens", tc_recv,
                 {"head": x * CORES + 1 - core})

        def token_to_partner(i):
            block = token_piece(half, h, i)
            send(block, block, "tokens", tz_recv.at[i], {"ctx": partner})

        def partner_tokens(i):
            arrived(token_piece(1 - half, h, i), tz_recv.at[i])
            spread(1 - half, 1, i)

        def pass_on(side, b, i):
            for d in range(1, n_x):
                block = token_piece(side, ((x + n_x - d) % n_x) * CORES + core, i)
                arrived(block, tx_recv.at[d, b, i])
                send(block, block, "tokens", tc_recv,
                     {"head": x * CORES + 1 - core})

        def wait_tokens():
            arrived(x_buf.at[pl.ds(0, n_tok // CORES), :], tc_recv)

        def send_stage(stage, kind):
            s = index(stage)
            src = source(stage, run)
            dst = piece(stage, z, run)
            if kind == "f":
                send(source(stage, 1 - run), piece(stage, z, 1 - run),
                     "weights", wy_recv.at[group(stage)], {"ctx": partner})
            elif kind == "p" or (kind == "h" and light):
                send(src, dst, "weights", wz_recv.at[s, z], {"ctx": partner})
            else:
                for k in range(1, n_pairs):
                    to = light_of(later_pair(k)) if kind == "l" else heavy_of(later_pair(k))
                    send(src, dst, "weights", wz_recv.at[s, z], {"ctx": to})

        def take(stage, src, relay=False, swap=True):
            s = index(stage)
            block = piece(stage, src, run)
            arrived(block, wz_recv.at[s, src])
            if relay:
                for k in range(1, n_pairs):
                    send(block, block, "weights", wz_recv.at[s, src],
                         {"ctx": heavy_of(later_pair(k))})
            if swap:
                send(block, block, "weights", wy_recv.at[group(stage)], other_run)

        def wait_weights(g, j):
            ref = q_w if j == QUERY else kv_w
            arrived(ref.at[unit(g), pl.ds(0, (n_ctx - 1) * rows_half), :], wy_recv.at[group((g, j))])

        def project(a_ref, b_ref, to_ref):
            def tile(step, carry):
                at = pl.ds(pl.multiple_of(step * WIDE_TILE, WIDE_TILE), WIDE_TILE)
                to_ref[at, :] = dot(a_ref[at, :], b_ref[...]).astype(jnp.bfloat16)
                return carry

            lax.fori_loop(0, n_tok // WIDE_TILE, tile, 0)

        def keys_values(g):
            u = unit(g)
            wait_weights(g, KEY)
            own_w[u * 3].wait()
            own_w[u * 3 + 1].wait()
            project(x_buf, kv_w.at[u], kv_buf.at[u])
            total = None
            for b in range(n_tok // BLOCK):
                here = pl.ds(b * BLOCK, BLOCK)
                one = dot(kv_buf[u, here, :dim], kv_buf[u, here, dim:], ((0,), (0,)))
                sums[u, b] = one
                total = one if total is None else total + one
            totals[u] = total.astype(totals.dtype)
            for k in range(1, n_pairs):
                @pl.when(pair + k < n_pairs)
                def _():
                    to = light_of(pair + k) if light else heavy_of(pair + k)
                    remote(totals.at[u], others.at[k, u], st_send.at[k, u], st_recv.at[k, u],
                           {"ctx": to}).start()

        def queries(g):
            u = unit(g)
            wait_weights(g, QUERY)
            own_w[u * 3 + 2].wait()
            project(x_buf, q_w.at[u], q_buf.at[u])

        def states(g):
            u = unit(g)
            for k in range(1, n_pairs):
                @pl.when(pair >= k)
                def _():
                    arrived(others.at[k, u], st_recv.at[k, u])
            state = prior_ref[g]
            for k in range(1, n_pairs):
                state = state + jnp.where(pair >= k, others[k, u].astype(jnp.float32), 0.0)
            for b in range(n_tok // BLOCK):
                starts[u, b] = state.astype(jnp.bfloat16)
                state = state + sums[u, b]

        def attend(g, side, bb, r):
            u = unit(g)
            b = side * per_span + bb
            base = pl.multiple_of(b * BLOCK, BLOCK)
            seen = r + TILE
            here = pl.ds(pl.multiple_of(base + r, TILE), TILE)
            before = pl.ds(base, seen)
            row = lax.broadcasted_iota(jnp.int32, (TILE, seen), 0) + r
            col = lax.broadcasted_iota(jnp.int32, (TILE, seen), 1)
            query = q_buf[u, here, :]
            scores = dot(query, kv_buf[u, before, :dim], ((1,), (1,)))
            scores = jnp.where(row >= col, scores, 0.0).astype(jnp.bfloat16)
            mixed = dot(scores, kv_buf[u, before, dim:]) + dot(query, starts[u, b])
            level = lax.rsqrt(jnp.mean(mixed * mixed, axis=-1, keepdims=True) + 1e-06)
            att[u, here, :] = (mixed * level * og_ref[g]).astype(jnp.bfloat16)

        def columns(head, g):
            return out_ref.at[:, pl.ds(pl.multiple_of((head * heads_here + g) * dim, dim), dim)]

        def outputs(g):
            u = unit(g)
            for bb in range(per_span):
                for r in range(0, BLOCK, TILE):
                    attend(g, 1 - half, bb, r)
                    first = (bb * BLOCK + r) // rows_here
                    for head in range(first, first + TILE // rows_here):
                        remote(att.at[u, slot(1 - half, head), :], columns(h, g),
                               o_send.at[u], o_recv, {"ctx": partner, "head": head}).start()
            for bb in range(per_span):
                for r in range(0, BLOCK, TILE):
                    attend(g, half, bb, r)
            for dh in range(1, n_head):
                to = (h + dh) % n_head
                remote(att.at[u, slot(half, to), :], columns(h, g),
                       o_send.at[u], o_recv, {"head": to}).start()
            pltpu.make_async_copy(att.at[u, slot(half, h), :], columns(h, g), o_own.at[u]).start()

        def step(time, work, *args):
            steps.append((time, len(steps), functools.partial(work, *args)))

        def by_head(g):
            return [s for s in H_STAGES if s[0] == g]

        def when(name, n, default=0.0):
            times = TIMES["L" if light else "H"].get(name)
            return times[min(n, len(times) - 1)] if times else default

        for n, stage in enumerate(my_stages):
            from_partner = when("LP" if light else "A", n)
            step(from_partner, take, stage, partner, not light,
                 light or not in_full(stage))
            for k in range(1, n_pairs):
                step(when("LH" if light else "B", n), take, stage, heavy_of(later_pair(k)))
                far = when("LL", n) if light else max(when("C", n), from_partner)
                step(far, take, stage, light_of(later_pair(k)))
        last = {}
        for time, _, work in steps:
            key = work.args[0][:2]
            last[key] = max(last.get(key, 0.0), time)
        free = 0.0
        for i in range(TOKEN_CUTS):
            near = when("TP", i)
            far = max(when("TF", i), near)
            step(near, partner_tokens, i)
            step(when("TX", i), pass_on, half, 0, i)
            step(far, pass_on, 1 - half, 1, i)
            free = max(free, far, when("TX", i))
        free = max(free, when("KV", 0))
        step(free, wait_tokens)
        for n, g in enumerate(my_heads):
            free = max(free, when("KV", n), last[g, KEY], last[g, VALUE])
            step(free, keys_values, g)
            free = max(free, when("Q", n), last[g, QUERY])
            step(free, queries, g)
            free = max(free, when("O1", n))
            step(free, states, g)
            step(free, outputs, g)

        def first(kind, n):
            if kind == "N":
                normalize()
            elif kind == "T":
                token_to_partner(n)
            elif kind == "X":
                spread(half, 0, n)
            else:
                send_stage((H_STAGES if kind in "hf" else L_STAGES)[n], kind)

        counts = {"N": 1, "T": TOKEN_CUTS, "X": TOKEN_CUTS, "h": len(H_STAGES),
                  "l": len(L_STAGES), "p": 0 if light else len(L_STAGES)}
        todo = [(name[0], int(name[1:] or 0)) for name in SENDS["L" if light else "H"]]
        todo = [(kind, n) for kind, n in todo if n < counts.get(kind, len(H_STAGES) if n_heavy > 1 else 0)]
        todo += [(kind, n) for kind in counts for n in range(counts[kind]) if (kind, n) not in todo]
        for kind, n in todo:
            first(kind, n)
        for copy in own_w:
            copy.start()
        loads[2].wait()
        loads[3].wait()
        for _, _, work in sorted(steps, key=lambda s: s[:2]):
            work()

        wait_sent("tokens", token_piece(half, h, 0))
        wait_sent("weights", piece(my_stages[0], z, run))
        for g in my_heads:
            u = unit(g)
            for k in range(1, n_pairs):
                @pl.when(pair + k < n_pairs)
                def _():
                    remote(totals.at[u], others.at[k, u], st_send.at[k, u], st_recv.at[k, u],
                           other_run).wait_send()
        for g in my_heads:
            u = unit(g)
            pltpu.make_async_copy(att.at[u, slot(half, h), :], columns(h, g), o_own.at[u]).wait()
            gone = att.at[u, pl.ds(0, (2 * n_head - 1) * rows_here), :]
            remote(gone, gone, o_send.at[u], o_recv, other_run).wait_send()
        n_there = n_head * heads_here - len(my_heads)
        arrived(out_ref.at[:, pl.ds(0, n_there * dim)], o_recv)

    @pl.when(is_light)
    def _():
        whole_program(True)

    @pl.when(jnp.logical_not(is_light))
    def _():
        whole_program(False)


def on_device(n_ctx, n_head, tokens, in_gain, projections, prior_state, out_gain):
    rows_here, features = tokens.shape
    heads_here, dim, _ = prior_state.shape
    n_heavy = heads_here - max(1, heads_here // 4)
    n_tok = 2 * n_head * rows_here
    n_blocks = n_tok // BLOCK
    n_x = n_head // CORES
    n_pairs = n_ctx // 2
    n_stages = 3 * heads_here
    dma = pltpu.SemaphoreType.DMA
    vmem = pl.BlockSpec(memory_space=pltpu.VMEM)
    bf16, f32 = jnp.bfloat16, jnp.float32
    return pl.pallas_call(
        functools.partial(kernel, n_ctx, n_head),
        out_shape=jax.ShapeDtypeStruct((rows_here, features), bf16),
        in_specs=[pl.BlockSpec(memory_space=pltpu.HBM)] * 5,
        out_specs=vmem,
        scratch_shapes=[
            pltpu.VMEM((rows_here, features), bf16),
            pltpu.VMEM((1, features), f32),
            pltpu.VMEM((heads_here, dim, dim), f32),
            pltpu.VMEM((heads_here, 1, dim), f32),
            dma((4 + 3 * n_heavy,)),
            pltpu.VMEM((n_tok, features), bf16),
            pltpu.VMEM((n_heavy, features, 2 * dim), bf16),
            pltpu.VMEM((n_heavy, features, dim), bf16),
            pltpu.VMEM((n_heavy, n_tok, 2 * dim), bf16),
            pltpu.VMEM((n_heavy, n_tok, dim), bf16),
            pltpu.VMEM((n_heavy, n_tok, dim), bf16),
            pltpu.VMEM((n_heavy, n_blocks, dim, dim), f32),
            pltpu.VMEM((n_heavy, dim, dim), STATE),
            pltpu.VMEM((n_pairs, n_heavy, dim, dim), STATE),
            pltpu.VMEM((n_heavy, n_blocks, dim, dim), bf16),
            dma,
            dma, dma((TOKEN_CUTS,)), dma((n_x, 2, TOKEN_CUTS)), dma,
            dma, dma((n_stages, n_ctx)), dma((2 * heads_here,)),
            dma((n_pairs, n_heavy)), dma((n_pairs, n_heavy)),
            dma((n_heavy,)), dma, dma((n_heavy,)),
        ],
        compiler_params=pltpu.CompilerParams(
            collective_id=0, has_side_effects=True, vmem_limit_bytes=60 * 1024 * 1024
        ),
    )(
        tokens,
        in_gain.reshape(1, features),
        projections,
        prior_state,
        out_gain.reshape(heads_here, 1, dim),
    )


def solution(mesh):
    in_specs = (
        P(("runs", "ctx", "head"), None),
        P(),
        P(None, "ctx", "head"),
        P(("runs", "head"), None, None),
        P("head"),
    )
    out_specs = P(("runs", "ctx", "head"), None)
    return jax.shard_map(
        functools.partial(on_device, mesh.shape["ctx"], mesh.shape["head"]),
        mesh=mesh, in_specs=in_specs, out_specs=out_specs, check_vma=False,
    )
```

```python
import functools

import jax
import jax.numpy as jnp
from jax import lax
from jax.experimental import pallas as pl
from jax.experimental.pallas import tpu as pltpu
from jax.sharding import PartitionSpec as P

BLOCK = 512
CORES = 2
MESH = pl.DeviceIdType.MESH
QUERY, KEY, VALUE = 0, 1, 2
TILE = 256
TOKEN_CUTS = 2
WIDE_TILE = 512
STATE = jnp.float32
SENDS = {
    "L": (
        "h0", "N", "T0", "X0", "X1", "h1", "T1", "h2", "h3", "l0", "h4", "h5",
        "l1", "l2", "h6", "f6", "h7", "f7", "h8", "f8",
    ),
    "H": (
        "h0", "h1", "N", "T0", "X0", "T1", "X1", "h2", "h3", "h4", "h5", "h6",
        "h7", "h8", "p0", "l0", "p1", "l1", "p2", "l2",
    ),
}
TIMES = {
    "H": {
        "A": (3.6, 10.7, 17.7, 19.1, 21.9, 23.3, 27.6, 31.3, 33.2,),
        "B": (3.7, 5.0, 6.4, 7.8, 9.4, 10.8, 12.1, 13.5, 14.9,),
        "C": (20.9, 23.5, 25.1, 27.9, 31.4, 32.6, 33.3, 37.3, 39.1,),
        "KV": (29.9, 35.9, 41.9,),
        "O1": (34.9, 40.9, 46.9,),
        "Q": (31.5, 37.4, 43.3,),
        "TF": (20.3, 25.9,),
        "TP": (9.2, 16.3,),
        "TX": (9.0, 14.7,),
    },
    "L": {
        "KV": (31.4,),
        "LH": (18.5, 21.3, 23.1,),
        "LL": (24.5, 27.7, 30.5,),
        "LP": (16.0, 18.8, 21.6,),
        "O1": (40.7,),
        "Q": (34.2,),
        "TF": (20.2, 25.9,),
        "TP": (9.0, 14.6,),
        "TX": (9.1, 14.7,),
    },
}


def dot(a, b, contract=((1,), (0,))):
    return lax.dot_general(a, b, (contract, ((), ())), preferred_element_type=jnp.float32)


def kernel(
    n_ctx, n_head,
    tok_hbm, gain_hbm, w_ref, prior_hbm, og_hbm,
    out_ref,
    tok_ref, gain_ref, prior_ref, og_ref, in_sems,
    x_buf, kv_w, q_w, kv_buf, q_buf, att, sums, totals, others, starts,
    own_sem, t_sent, tz_recv, tx_recv, tc_recv,
    w_sent, wz_recv, wy_recv, st_send, st_recv, o_send, o_recv, o_own,
):
    run = lax.axis_index("runs")
    z = lax.axis_index("ctx")
    h = lax.axis_index("head")
    n_x = n_head // CORES
    x, core = h // CORES, h % CORES
    half = z % 2
    pair = z // 2
    n_pairs = n_ctx // 2
    partner = z + 1 - 2 * half
    other_run = {"runs": 1 - run}
    rows_here = tok_ref.shape[0]
    rows = w_ref.shape[1]
    rows_half = rows // 2
    heads_here, dim, _ = prior_ref.shape
    n_heavy = kv_w.shape[0]
    n_light = heads_here - n_heavy
    n_tok = x_buf.shape[0]
    span = n_tok // 2
    per_span = span // BLOCK
    tok_cut = rows_here // TOKEN_CUTS

    is_light = half == pair % 2

    def light_of(q):
        return 2 * q + q % 2

    def heavy_of(q):
        return 2 * q + 1 - q % 2

    def later_pair(k):
        return (pair + k) % n_pairs

    L_HEADS = list(range(n_light))
    H_HEADS = list(range(n_light, heads_here))
    L_STAGES = [(g, j) for g in L_HEADS for j in (KEY, VALUE, QUERY)]
    H_STAGES = [(g, j) for g in H_HEADS for j in (KEY, VALUE, QUERY)]

    def unit(g):
        return g if g < n_light else g - n_light

    def index(stage):
        return stage[0] * 3 + stage[1]

    def group(stage):
        return stage[0] * 2 + (stage[1] == QUERY)

    def in_full(stage):
        return n_heavy > 1 and "f%d" % H_STAGES.index(stage) in SENDS["L"]

    def slot(side, head):
        return pl.ds(pl.multiple_of((side * n_head + head) * rows_here, rows_here), rows_here)

    def token_piece(side, head, i):
        start = (side * n_head + head) * rows_here + i * tok_cut
        return x_buf.at[pl.ds(pl.multiple_of(start, tok_cut), tok_cut), :]

    def source(stage, part):
        g, j = stage
        start = pl.multiple_of(part * rows_half, rows_half)
        return w_ref.at[j, pl.ds(start, rows_half), pl.ds(g * dim, dim)]

    def place(g, j, at):
        u = unit(g)
        if j == QUERY:
            return q_w.at[u, at, :]
        return kv_w.at[u, at, pl.ds((j - KEY) * dim, dim)]

    def piece(stage, src, part):
        start = pl.multiple_of(src * rows + part * rows_half, rows_half)
        return place(*stage, pl.ds(start, rows_half))

    loads = [
        pltpu.make_async_copy(src, dst, in_sems.at[n])
        for n, (src, dst) in enumerate((
            (tok_hbm, tok_ref), (gain_hbm, gain_ref), (prior_hbm, prior_ref), (og_hbm, og_ref),
        ))
    ]
    for load in loads:
        load.start()

    barrier = pltpu.get_barrier_semaphore()
    greeted = [other_run]
    greeted += [{"ctx": (z + k) % n_ctx} for k in range(1, n_ctx)]
    greeted += [{"head": (h + k) % n_head} for k in range(1, n_head)]
    greeted += [{"ctx": partner, "head": (h + k) % n_head} for k in range(1, n_head)]
    for device in greeted:
        pl.semaphore_signal(barrier, inc=1, device_id=device, device_id_type=MESH)

    pl.semaphore_wait(barrier, len(greeted))

    def normalize():
        loads[0].wait()
        loads[1].wait()
        wide = tok_ref[...].astype(jnp.float32)
        scale = lax.rsqrt(jnp.mean(wide * wide, axis=-1, keepdims=True) + 1e-06)
        x_buf[slot(half, h), :] = (wide * scale * gain_ref[...]).astype(jnp.bfloat16)

    def remote(src, dst, send_sem, recv_sem, device):
        return pltpu.make_async_remote_copy(
            src_ref=src, dst_ref=dst, send_sem=send_sem, recv_sem=recv_sem,
            device_id=device, device_id_type=MESH,
        )

    def arrived(dst, recv_sem):
        remote(dst, dst, own_sem, recv_sem, other_run).wait_recv()

    sent_sems = {"tokens": t_sent, "weights": w_sent}

    def whole_program(light):
        my_heads = L_HEADS if light else H_HEADS
        my_stages = L_STAGES if light else H_STAGES
        steps = []
        n_sent = {"tokens": 0, "weights": 0}

        def send(src, dst, kind, recv_sem, device):
            remote(src, dst, sent_sems[kind], recv_sem, device).start()
            n_sent[kind] += 1

        def wait_sent(kind, ref):
            copies = n_sent[kind] * (ref.shape[0] * ref.shape[1])
            whole = copies // x_buf.shape[1]
            if whole <= n_tok and whole % 16 == 0 and whole * x_buf.shape[1] == copies:
                ref, times = x_buf.at[pl.ds(0, whole), :], 1
            else:
                times = n_sent[kind]
            for _ in range(times):
                remote(ref, ref, sent_sems[kind], own_sem, other_run).wait_send()

        own_w = [
            pltpu.make_async_copy(
                w_ref.at[j, :, pl.ds(g * dim, dim)],
                place(g, j, pl.ds(pl.multiple_of(z * rows, rows), rows)),
                in_sems.at[4 + unit(g) * 3 + j],
            )
            for g in my_heads for j in (KEY, VALUE, QUERY)
        ]

        def spread(side, b, i):
            block = token_piece(side, h, i)
            for d in range(1, n_x):
                send(block, block, "tokens", tx_recv.at[d, b, i],
                     {"head": ((x + d) % n_x) * CORES + core})
            if b == 1:
                send(block, block, "tokens", tc_recv, {"head": x * CORES + 1 - core})
            elif i == 0:
                block = x_buf.at[slot(side, h), :]
                send(block, block, "tokens", tc_recv, {"head": x * CORES + 1 - core})
                n_sent["tokens"] += TOKEN_CUTS - 1

        def token_to_partner(i):
            block = token_piece(half, h, i)
            send(block, block, "tokens", tz_recv.at[i], {"ctx": partner})

        def partner_tokens(i):
            arrived(token_piece(1 - half, h, i), tz_recv.at[i])
            spread(1 - half, 1, i)

        def pass_on(side, b, i):
            for d in range(1, n_x):
                block = token_piece(side, ((x + n_x - d) % n_x) * CORES + core, i)
                arrived(block, tx_recv.at[d, b, i])
                send(block, block, "tokens", tc_recv,
                     {"head": x * CORES + 1 - core})

        def wait_tokens():
            arrived(x_buf.at[pl.ds(0, n_tok // CORES), :], tc_recv)

        def send_stage(stage, kind):
            s = index(stage)
            src = source(stage, run)
            dst = piece(stage, z, run)
            if kind == "f":
                send(source(stage, 1 - run), piece(stage, z, 1 - run),
                     "weights", wy_recv.at[group(stage)], {"ctx": partner})
            elif kind == "p" or (kind == "h" and light):
                send(src, dst, "weights", wz_recv.at[s, z], {"ctx": partner})
            else:
                for k in range(1, n_pairs):
                    to = light_of(later_pair(k)) if kind == "l" else heavy_of(later_pair(k))
                    send(src, dst, "weights", wz_recv.at[s, z], {"ctx": to})

        def take(stage, src, relay=False, swap=True):
            s = index(stage)
            block = piece(stage, src, run)
            arrived(block, wz_recv.at[s, src])
            if relay:
                for k in range(1, n_pairs):
                    send(block, block, "weights", wz_recv.at[s, src],
                         {"ctx": heavy_of(later_pair(k))})
            if swap:
                send(block, block, "weights", wy_recv.at[group(stage)], other_run)

        def wait_weights(g, j):
            ref = q_w if j == QUERY else kv_w
            arrived(ref.at[unit(g), pl.ds(0, (n_ctx - 1) * rows_half), :], wy_recv.at[group((g, j))])

        def project(a_ref, b_ref, to_ref):
            def tile(step, carry):
                at = pl.ds(pl.multiple_of(step * WIDE_TILE, WIDE_TILE), WIDE_TILE)
                to_ref[at, :] = dot(a_ref[at, :], b_ref[...]).astype(jnp.bfloat16)
                return carry

            lax.fori_loop(0, n_tok // WIDE_TILE, tile, 0)

        def keys_values(g):
            u = unit(g)
            wait_weights(g, KEY)
            own_w[u * 3].wait()
            own_w[u * 3 + 1].wait()
            project(x_buf, kv_w.at[u], kv_buf.at[u])
            total = None
            for b in range(n_tok // BLOCK):
                here = pl.ds(b * BLOCK, BLOCK)
                one = dot(kv_buf[u, here, :dim], kv_buf[u, here, dim:], ((0,), (0,)))
                sums[u, b] = one
                total = one if total is None else total + one
            totals[u] = total.astype(totals.dtype)
            for k in range(1, n_pairs):
                @pl.when(pair + k < n_pairs)
                def _():
                    to = light_of(pair + k) if light else heavy_of(pair + k)
                    remote(totals.at[u], others.at[k, u], st_send.at[k, u], st_recv.at[k, u],
                           {"ctx": to}).start()

        def queries(g):
            u = unit(g)
            wait_weights(g, QUERY)
            own_w[u * 3 + 2].wait()
            project(x_buf, q_w.at[u], q_buf.at[u])

        def states(g):
            u = unit(g)
            for k in range(1, n_pairs):
                @pl.when(pair >= k)
                def _():
                    arrived(others.at[k, u], st_recv.at[k, u])
            state = prior_ref[g]
            for k in range(1, n_pairs):
                state = state + jnp.where(pair >= k, others[k, u].astype(jnp.float32), 0.0)
            for b in range(n_tok // BLOCK):
                starts[u, b] = state.astype(jnp.bfloat16)
                state = state + sums[u, b]

        def attend(g, side, bb, r):
            u = unit(g)
            b = side * per_span + bb
            base = pl.multiple_of(b * BLOCK, BLOCK)
            seen = r + TILE
            here = pl.ds(pl.multiple_of(base + r, TILE), TILE)
            before = pl.ds(base, seen)
            row = lax.broadcasted_iota(jnp.int32, (TILE, seen), 0) + r
            col = lax.broadcasted_iota(jnp.int32, (TILE, seen), 1)
            query = q_buf[u, here, :]
            scores = dot(query, kv_buf[u, before, :dim], ((1,), (1,)))
            scores = jnp.where(row >= col, scores, 0.0).astype(jnp.bfloat16)
            mixed = dot(scores, kv_buf[u, before, dim:]) + dot(query, starts[u, b])
            level = lax.rsqrt(jnp.mean(mixed * mixed, axis=-1, keepdims=True) + 1e-06)
            att[u, here, :] = (mixed * level * og_ref[g]).astype(jnp.bfloat16)

        def columns(head, g):
            return out_ref.at[:, pl.ds(pl.multiple_of((head * heads_here + g) * dim, dim), dim)]

        def outputs(g):
            u = unit(g)
            for bb in range(per_span):
                for r in range(0, BLOCK, TILE):
                    attend(g, 1 - half, bb, r)
                    first = (bb * BLOCK + r) // rows_here
                    for head in range(first, first + TILE // rows_here):
                        remote(att.at[u, slot(1 - half, head), :], columns(h, g),
                               o_send.at[u], o_recv, {"ctx": partner, "head": head}).start()
            for bb in range(per_span):
                for r in range(0, BLOCK, TILE):
                    attend(g, half, bb, r)
            for dh in range(1, n_head):
                to = (h + dh) % n_head
                remote(att.at[u, slot(half, to), :], columns(h, g),
                       o_send.at[u], o_recv, {"head": to}).start()
            pltpu.make_async_copy(att.at[u, slot(half, h), :], columns(h, g), o_own.at[u]).start()

        def step(time, work, *args):
            steps.append((time, len(steps), functools.partial(work, *args)))

        def by_head(g):
            return [s for s in H_STAGES if s[0] == g]

        def when(name, n, default=0.0):
            times = TIMES["L" if light else "H"].get(name)
            return times[min(n, len(times) - 1)] if times else default

        for n, stage in enumerate(my_stages):
            from_partner = when("LP" if light else "A", n)
            step(from_partner, take, stage, partner, not light,
                 light or not in_full(stage))
            for k in range(1, n_pairs):
                step(when("LH" if light else "B", n), take, stage, heavy_of(later_pair(k)))
                far = when("LL", n) if light else max(when("C", n), from_partner)
                step(far, take, stage, light_of(later_pair(k)))
        last = {}
        for time, _, work in steps:
            key = work.args[0][:2]
            last[key] = max(last.get(key, 0.0), time)
        free = 0.0
        for i in range(TOKEN_CUTS):
            near = when("TP", i)
            far = max(when("TF", i), near)
            step(near, partner_tokens, i)
            step(when("TX", i), pass_on, half, 0, i)
            step(far, pass_on, 1 - half, 1, i)
            free = max(free, far, when("TX", i))
        free = max(free, when("KV", 0))
        step(free, wait_tokens)
        for n, g in enumerate(my_heads):
            free = max(free, when("KV", n), last[g, KEY], last[g, VALUE])
            step(free, keys_values, g)
            free = max(free, when("Q", n), last[g, QUERY])
            step(free, queries, g)
            free = max(free, when("O1", n))
            step(free, states, g)
            step(free, outputs, g)

        def first(kind, n):
            if kind == "N":
                normalize()
            elif kind == "T":
                token_to_partner(n)
            elif kind == "X":
                spread(half, 0, n)
            else:
                send_stage((H_STAGES if kind in "hf" else L_STAGES)[n], kind)

        counts = {"N": 1, "T": TOKEN_CUTS, "X": TOKEN_CUTS, "h": len(H_STAGES),
                  "l": len(L_STAGES), "p": 0 if light else len(L_STAGES)}
        todo = [(name[0], int(name[1:] or 0)) for name in SENDS["L" if light else "H"]]
        todo = [(kind, n) for kind, n in todo if n < counts.get(kind, len(H_STAGES) if n_heavy > 1 else 0)]
        todo += [(kind, n) for kind in counts for n in range(counts[kind]) if (kind, n) not in todo]
        for kind, n in todo:
            first(kind, n)
        for copy in own_w:
            copy.start()
        loads[2].wait()
        loads[3].wait()
        for _, _, work in sorted(steps, key=lambda s: s[:2]):
            work()

        wait_sent("tokens", token_piece(half, h, 0))
        wait_sent("weights", piece(my_stages[0], z, run))
        for g in my_heads:
            u = unit(g)
            for k in range(1, n_pairs):
                @pl.when(pair + k < n_pairs)
                def _():
                    remote(totals.at[u], others.at[k, u], st_send.at[k, u], st_recv.at[k, u],
                           other_run).wait_send()
        for g in my_heads:
            u = unit(g)
            pltpu.make_async_copy(att.at[u, slot(half, h), :], columns(h, g), o_own.at[u]).wait()
            gone = att.at[u, pl.ds(0, (2 * n_head - 1) * rows_here), :]
            remote(gone, gone, o_send.at[u], o_recv, other_run).wait_send()
        n_there = n_head * heads_here - len(my_heads)
        arrived(out_ref.at[:, pl.ds(0, n_there * dim)], o_recv)

    @pl.when(is_light)
    def _():
        whole_program(True)

    @pl.when(jnp.logical_not(is_light))
    def _():
        whole_program(False)


def on_device(n_ctx, n_head, tokens, in_gain, projections, prior_state, out_gain):
    rows_here, features = tokens.shape
    heads_here, dim, _ = prior_state.shape
    n_heavy = heads_here - max(1, heads_here // 4)
    n_tok = 2 * n_head * rows_here
    n_blocks = n_tok // BLOCK
    n_x = n_head // CORES
    n_pairs = n_ctx // 2
    n_stages = 3 * heads_here
    dma = pltpu.SemaphoreType.DMA
    vmem = pl.BlockSpec(memory_space=pltpu.VMEM)
    bf16, f32 = jnp.bfloat16, jnp.float32
    return pl.pallas_call(
        functools.partial(kernel, n_ctx, n_head),
        out_shape=jax.ShapeDtypeStruct((rows_here, features), bf16),
        in_specs=[pl.BlockSpec(memory_space=pltpu.HBM)] * 5,
        out_specs=vmem,
        scratch_shapes=[
            pltpu.VMEM((rows_here, features), bf16),
            pltpu.VMEM((1, features), f32),
            pltpu.VMEM((heads_here, dim, dim), f32),
            pltpu.VMEM((heads_here, 1, dim), f32),
            dma((4 + 3 * n_heavy,)),
            pltpu.VMEM((n_tok, features), bf16),
            pltpu.VMEM((n_heavy, features, 2 * dim), bf16),
            pltpu.VMEM((n_heavy, features, dim), bf16),
            pltpu.VMEM((n_heavy, n_tok, 2 * dim), bf16),
            pltpu.VMEM((n_heavy, n_tok, dim), bf16),
            pltpu.VMEM((n_heavy, n_tok, dim), bf16),
            pltpu.VMEM((n_heavy, n_blocks, dim, dim), f32),
            pltpu.VMEM((n_heavy, dim, dim), STATE),
            pltpu.VMEM((n_pairs, n_heavy, dim, dim), STATE),
            pltpu.VMEM((n_heavy, n_blocks, dim, dim), bf16),
            dma,
            dma, dma((TOKEN_CUTS,)), dma((n_x, 2, TOKEN_CUTS)), dma,
            dma, dma((n_stages, n_ctx)), dma((2 * heads_here,)),
            dma((n_pairs, n_heavy)), dma((n_pairs, n_heavy)),
            dma((n_heavy,)), dma, dma((n_heavy,)),
        ],
        compiler_params=pltpu.CompilerParams(
            collective_id=0, has_side_effects=True, vmem_limit_bytes=60 * 1024 * 1024
        ),
    )(
        tokens,
        in_gain.reshape(1, features),
        projections,
        prior_state,
        out_gain.reshape(heads_here, 1, dim),
    )


def solution(mesh):
    in_specs = (
        P(("runs", "ctx", "head"), None),
        P(),
        P(None, "ctx", "head"),
        P(("runs", "head"), None, None),
        P("head"),
    )
    out_specs = P(("runs", "ctx", "head"), None)
    return jax.shard_map(
        functools.partial(on_device, mesh.shape["ctx"], mesh.shape["head"]),
        mesh=mesh, in_specs=in_specs, out_specs=out_specs, check_vma=False,
    )
```
